32 devices in a mesh: row: 4 (over y, x), col: 8 (over z, core).
Axes of the slice: x: 2, y: 2, z: 4, core: 2. Of those that a mesh axis runs over, the one named last changes fastest.
Arguments:
- train_inputs: bfloat16 [512, 8192], P(('row', 'col')), may hold values from -6 to 6
- train_grads: bfloat16 [512, 8192], P(('row', 'col')), may hold values from -6 to 6
- query_inputs: bfloat16 [256, 8192], P(('row', 'col')), may hold values from -6 to 6
- query_grads: bfloat16 [256, 8192], P(('row', 'col')), may hold values from -6 to 6
- input_basis: bfloat16 [8192, 8192], P('row', 'col'), may hold values from -0.0625 to 0.0625
- output_basis: bfloat16 [8192, 8192], P('col', 'row'), may hold values from -0.0625 to 0.0625
- eigenvalues: float32 [8192, 8192], P('row', 'col'), may hold values from 0.5 to 5
- query_starts: int32 [16], replicated, may hold values from 0 to 255, as said below
- query_ends: int32 [16], replicated, may hold values from 1 to 256, as said below
Outputs:
- scores: float32 [16, 512], replicated
The draws below stay inside these ranges and needn't reach their ends.
Inputs may be any that keep to these rules, and one draw needn't show every extreme that they name: Query q covers the query rows query_starts[q] <= r < query_ends[q]: a nonempty span of at most 128 rows that lies inside one aligned block of 128 rows (rows k * 128 to (k + 1) * 128 - 1); spans of different queries may intersect or share a block. `query_ends`: see query_starts.
All inputs are finite; a program needn't handle non-finite values.
Results may differ from the reference program's by a relative error of at most 0.005.
Values may be sent and summed in bfloat16 or wider, within the bound.
No kernel may reach another device: no remote copies, remote signals or barrier semaphores. Data moves between devices by JAX's collectives and lax.ppermute only.
A program may use at most 64 MiB of HBM per device.

```python
import math
import jax
import jax.numpy as jnp
from jax import lax

D_IN = 8192
D_OUT = 8192
TRAIN = 512
QROWS = 256
NQ = 16
QBLOCK = 128


def query_spans(key):
    keys = jax.random.split(jax.random.fold_in(key, 7), 3)
    blocks = jax.random.randint(keys[0], (NQ,), 0, QROWS // QBLOCK)
    offsets = jax.random.randint(keys[1], (NQ,), 0, QBLOCK)
    lengths = jax.random.randint(keys[2], (NQ,), 1, QBLOCK - offsets + 1)
    which = jnp.arange(NQ, dtype=jnp.int32)
    blocks = jnp.where(which == 0, QROWS // QBLOCK - 1, blocks)
    offsets = jnp.where(which <= 1, 0, offsets)
    lengths = jnp.where(which == 0, QBLOCK, lengths)
    starts = blocks * QBLOCK + offsets
    return (starts.astype(jnp.int32), (starts + lengths).astype(jnp.int32))


def draw_query_starts(key, part):
    return query_spans(key)[0]


def draw_query_ends(key, part):
    return query_spans(key)[1]


def shard_levels(own_key, shape, shards, least, largest):
    level, own = 1.0, jax.random.fold_in(own_key, 6)
    for position, shards_of in shards:
        heights = jnp.exp(jax.random.uniform(jax.random.fold_in(own, position), (shards_of,), jnp.float32, least / len(shards), largest / len(shards)))
        level = level * jnp.repeat(heights, shape[position] // shards_of).reshape([-1 if axis == position else 1 for axis in range(len(shape))])
    return level


def bell_draw(rng, shape, scale, bound, cuts=(), held_as=jnp.bfloat16):
    drawn = scale * jax.random.normal(rng, shape, jnp.float32)
    if cuts:
        drawn = drawn * shard_levels(rng, shape, cuts, -0.22, 0.18)
    return jnp.clip(drawn, -bound, bound).astype(held_as)


def setup_inputs(seed: int = 0) -> dict:
    seeds = jax.random.split(jax.random.key(seed), 10)
    return {
        "train_inputs": bell_draw(seeds[0], (TRAIN, D_IN), 1.0, 6.0, ((0, 32),)),
        "train_grads": bell_draw(seeds[1], (TRAIN, D_OUT), 1.0, 6.0, ((0, 32),)),
        "query_inputs": bell_draw(seeds[2], (QROWS, D_IN), 1.0, 6.0, ((0, 32),)),
        "query_grads": bell_draw(seeds[3], (QROWS, D_OUT), 1.0, 6.0, ((0, 32),)),
        "input_basis": bell_draw(seeds[4], (D_IN, D_IN), D_IN ** -0.5, 0.0625, ((0, 4), (1, 8))),
        "output_basis": bell_draw(seeds[5], (D_OUT, D_OUT), D_OUT ** -0.5, 0.0625, ((0, 8), (1, 4))),
        "eigenvalues": jnp.clip(jnp.exp(math.log(5.0) - 2.3025851 * jax.random.uniform(seeds[6], (D_OUT, D_IN), jnp.float32) ** shard_levels(seeds[6], (D_OUT, D_IN), ((0, 4), (1, 8)), -0.2, 0.2)), 0.5, 5.0),
        "query_starts": draw_query_starts(jax.random.fold_in(seeds[9], 71), 0),
        "query_ends": draw_query_ends(jax.random.fold_in(seeds[9], 71), 0),
    }


damping = 0.1

def rotate(rows, basis):
    return jnp.dot(rows, basis, preferred_element_type=jnp.float32).astype(jnp.bfloat16)

def reference(train_inputs, train_grads, query_inputs, query_grads, input_basis, output_basis, eigenvalues, query_starts, query_ends):
    train_in_rot = rotate(train_inputs, input_basis)
    query_in_rot = rotate(query_inputs, input_basis)
    train_grad_rot = rotate(train_grads, output_basis)
    query_grad_rot = rotate(query_grads, output_basis)
    grads_wide = train_grad_rot.astype(jnp.float32)
    denominator = eigenvalues + damping

    def per_query(span):
        span_start, span_end = span
        block_top = span_start // QBLOCK * QBLOCK
        grad_rows = lax.dynamic_slice_in_dim(query_grad_rot, block_top, QBLOCK, 0)
        input_rows = lax.dynamic_slice_in_dim(query_in_rot, block_top, QBLOCK, 0)
        positions = block_top + jnp.arange(QBLOCK, dtype=jnp.int32)
        inside = (positions >= span_start) & (positions < span_end)
        grad_rows = jnp.where(inside[:, None], grad_rows, jnp.zeros((), grad_rows.dtype))
        outer_sum = lax.dot_general(grad_rows, input_rows, (((0,), (0,)), ((), ())), preferred_element_type=jnp.float32)
        scaled = (outer_sum / denominator).astype(jnp.bfloat16)
        paired = lax.dot_general(train_in_rot, scaled, (((1,), (1,)), ((), ())), preferred_element_type=jnp.float32)
        return lax.optimization_barrier(jnp.sum(grads_wide * paired, axis=1))
    totals = lax.map(per_query, (query_starts, query_ends))
    return totals * (1.0 / math.sqrt(D_IN * D_OUT * QBLOCK))
```

```python
import functools
import math

import jax
import jax.numpy as jnp
from jax import lax
from jax.experimental import pallas as pl
from jax.experimental.pallas import tpu as pltpu
from jax.sharding import PartitionSpec as P


QBLOCK = 128
CHUNKS = (1, 1)
GROUPS = 2
damping = 0.1
bf16, f32 = jnp.bfloat16, jnp.float32


def swap(x, axis, k):
    if k == 0:
        return x
    return lax.ppermute(x, axis, [(i, i ^ k) for i in range(lax.axis_size(axis))])


def tree_sum(parts):
    while len(parts) > 1:
        parts = [parts[i] + parts[i + 1] for i in range(0, len(parts), 2)]
    return parts[0]


def global_rows(index, own, R, C, a, b):
    device, row = index // own, index % own
    return ((((device % R) ^ a) * C) + ((device // R) ^ b)) * own + row


def score_kernel(spans, ti_ref, qi_ref, *refs, n_queries, sizes, first, last):
    R, C, nt, nq = sizes
    if not first:
        init_ref, *refs = refs
    eig_ref, *refs = refs
    pieces, (out_ref, tiT_ref, d_ref, acc_ref) = refs[:C], refs[C:]
    step = pl.program_id(0)
    a, b = spans[2 * n_queries], spans[2 * n_queries + 1]

    @pl.when(step == 0)
    def _():
        acc_ref[...] = jnp.zeros_like(acc_ref)
        tiT_ref[...] = ti_ref[...].T

    d_ref[...] = 1.0 / (eig_ref[...] + damping)
    tg = jnp.concatenate([p[:R * nt, :] for p in pieces], axis=0).T.astype(f32)
    qg = jnp.concatenate([p[R * nt:, :] for p in pieces], axis=0).T
    pos = global_rows(lax.broadcasted_iota(jnp.int32, (1, R * C * nq), 1), nq, R, C, a, b)
    for q in range(n_queries):
        inside = (pos >= spans[q]) & (pos < spans[n_queries + q])
        mask = jnp.where(inside, 1.0, 0.0).astype(bf16)
        outer = jnp.dot(qg * mask, qi_ref[...], preferred_element_type=f32)
        scaled = (outer * d_ref[...]).astype(bf16)
        paired = jnp.dot(scaled, tiT_ref[...], preferred_element_type=f32)
        v = paired * tg
        acc_ref[q] += v.reshape(v.shape[0] // 8, 8, v.shape[1]).sum(0)

    @pl.when(step == pl.num_programs(0) - 1)
    def _():
        total = acc_ref[...].sum(1)
        if not first:
            total = total + init_ref[...]
        if last:
            n = total.shape[1]
            rows = global_rows(lax.broadcasted_iota(jnp.int32, (n, n), 0), nt, R, C, a, b)
            cols = lax.broadcasted_iota(jnp.int32, (n, n), 1)
            onehot = jnp.where(rows == cols, 1.0, 0.0).astype(f32)
            total = jnp.dot(total, onehot, preferred_element_type=f32, precision=lax.Precision.HIGHEST)
        out_ref[...] = total


def score(spans, ti, qi, init, eig, pieces, start, n_queries, sizes, last, block=256):
    T, I = ti.shape
    rows, width = pieces[0].shape
    block = min(block, width)
    whole = lambda arr: pl.BlockSpec(arr.shape, lambda i, *_: (0, 0))
    init = [] if init is None else [init]
    return pl.pallas_call(
        functools.partial(score_kernel, n_queries=n_queries, sizes=sizes, first=not init, last=last),
        out_shape=jax.ShapeDtypeStruct((n_queries, T), f32),
        grid_spec=pltpu.PrefetchScalarGridSpec(
            num_scalar_prefetch=1,
            grid=(width // block,),
            in_specs=[
                whole(ti), whole(qi), *map(whole, init),
                pl.BlockSpec((block, I), lambda i, *_: (start // block + i, 0)),
                *[pl.BlockSpec((rows, block), lambda i, *_: (0, i)) for _ in pieces],
            ],
            out_specs=pl.BlockSpec((n_queries, T), lambda i, *_: (0, 0)),
            scratch_shapes=[
                pltpu.VMEM((I, T), bf16),
                pltpu.VMEM((block, I), f32),
                pltpu.VMEM((n_queries, 8, T), f32),
            ],
        ),
        compiler_params=pltpu.CompilerParams(
            dimension_semantics=("arbitrary",), vmem_limit_bytes=56 << 20),
    )(spans, ti, qi, *init, eig, *pieces)


def shards(
    train_inputs,
    train_grads,
    query_inputs,
    query_grads,
    input_basis,
    output_basis,
    eigenvalues,
    query_starts,
    query_ends,
):
    R, C = lax.axis_size("row"), lax.axis_size("col")
    Z = C // 2
    a, b = lax.axis_index("row"), lax.axis_index("col")
    nt, nq = train_inputs.shape[0], query_inputs.shape[0]
    n = nt + nq
    K_in, I = input_basis.shape
    K_out, O = output_basis.shape
    n_queries = query_starts.shape[0]

    spans = jnp.concatenate([query_starts, query_ends, jnp.stack([a, b]).astype(jnp.int32)])

    x_in = jnp.concatenate([train_inputs, query_inputs], axis=0)
    in_a = [swap(lax.dynamic_slice_in_dim(x_in, (a ^ k) * K_in, K_in, 1), "row", k) for k in range(R)]
    x_out = jnp.concatenate([train_grads, query_grads], axis=0)
    parts = [lax.dynamic_slice_in_dim(x_out, (b ^ k) * K_out, K_out, 1) for k in range(C)]
    other = swap(jnp.concatenate(parts[1::2], axis=0), "col", 1)
    out_a = [swap(jnp.concatenate([parts[2 * z], other[z * n:(z + 1) * n]], axis=0), "col", 2 * z) for z in range(Z)]

    in_a = jnp.concatenate(in_a, axis=0)
    in_z = [swap(in_a, "col", 2 * z) for z in range(Z)]
    in_c = [swap(p, "col", 1) for p in in_z]
    out_a = jnp.concatenate(out_a, axis=0)
    out_r = [swap(out_a, "row", k) for k in range(R)]

    zs = Z // GROUPS

    def send_inputs(g):
        pieces = [p for z in range(g * zs, (g + 1) * zs) for p in (in_z[z], in_c[z])]
        rows = jnp.stack([p.reshape(R, n, K_in) for p in pieces], axis=1).reshape(R, 2 * zs * n, K_in)
        parts = []
        for k in range(R):
            parts.append(jnp.dot(rows[k], input_basis, preferred_element_type=f32))
        return [parts[0]] + [swap(parts[k], "row", k) for k in range(1, R)]

    def share_inputs(got):
        total = tree_sum(got).astype(bf16)
        return [swap(total, "row", k).reshape(2 * zs, n, I) for k in range(R)]

    def grad_rows():
        stacked = jnp.stack(out_r, axis=0).reshape(R, Z, 2, n, K_out)

        def half(rcore):
            h = stacked[:, :, rcore]
            t = h[:, :, :nt].transpose(1, 0, 2, 3).reshape(Z, R * nt, K_out)
            q = h[:, :, nt:].transpose(1, 0, 2, 3).reshape(Z, R * nq, K_out)
            return jnp.concatenate([t, q], axis=1).reshape(Z * R * n, K_out)

        return half(0), half(1)

    starts = [sum(CHUNKS[:c]) * O // sum(CHUNKS) for c in range(len(CHUNKS) + 1)]

    def send_grads(c, mine, other):
        basis = output_basis[:, starts[c]:starts[c + 1]]
        sent = jnp.dot(other, basis, preferred_element_type=f32)
        got = swap(sent, "col", 1)
        kept = jnp.dot(mine, basis, preferred_element_type=f32)
        both = (kept + got).reshape(Z, R * n, -1)
        parts = [both[0]] + [both[z].astype(bf16) for z in range(1, Z)]
        return [swap(p, "col", 2 * z) for z, p in enumerate(parts)]

    def share_grads(got):
        got = [got[0]] + [p.astype(f32) for p in got[1:]]
        total = tree_sum(got).astype(bf16)
        own = [swap(total, "col", 2 * z) for z in range(Z)]
        theirs = [swap(p, "col", 1) for p in own]
        return [p for two in zip(own, theirs) for p in two]

    in_got = [send_inputs(g) for g in range(GROUPS)]
    mine, other = grad_rows()
    sums = [send_grads(c, mine, other) for c in range(len(CHUNKS))]
    shared = [share_inputs(got) for got in in_got]
    grad_pieces = [share_grads(got) for got in sums]
    ti = jnp.concatenate([jnp.stack([p[:, :nt] for p in rot], axis=1) for rot in shared], axis=0)
    qi = jnp.concatenate([jnp.stack([p[:, nt:] for p in rot], axis=1) for rot in shared], axis=0)
    ti, qi = ti.reshape(R * C * nt, I), qi.reshape(R * C * nq, I)

    scores = None
    for c in range(len(CHUNKS)):
        scores = score(spans, ti, qi, scores, eigenvalues, grad_pieces[c], starts[c],
                       n_queries, (R, C, nt, nq), c == len(CHUNKS) - 1)

    scores = scores + swap(scores, "col", 1)
    scores = tree_sum([swap(scores, "col", 2 * z) for z in range(Z)])
    scores = tree_sum([swap(scores, "row", k) for k in range(R)])
    return scores * (1.0 / math.sqrt(K_in * R * O * R * QBLOCK))


def solution(mesh):
    in_specs = (
        P(("row", "col"), None),
        P(("row", "col"), None),
        P(("row", "col"), None),
        P(("row", "col"), None),
        P("row", "col"),
        P("col", "row"),
        P("row", "col"),
        P(),
        P(),
    )

    return jax.shard_map(shards, mesh=mesh, in_specs=in_specs, out_specs=P(), check_vma=False)
```

```python
import functools
import math

import jax
import jax.numpy as jnp
from jax import lax
from jax.experimental import pallas as pl
from jax.experimental.pallas import tpu as pltpu
from jax.sharding import PartitionSpec as P


QBLOCK = 128
CHUNKS = (3, 5)
GROUPS = (1, 1)
SHARES = ((0,), (1,))
damping = 0.1
bf16, f32 = jnp.bfloat16, jnp.float32


def swap(x, axis, k):
    if k == 0:
        return x
    return lax.ppermute(x, axis, [(i, i ^ k) for i in range(lax.axis_size(axis))])


def gather(x, axis, unit):
    pieces = [x]
    for k in range(1, lax.axis_size(axis) // unit):
        low = k & -k
        pieces.append(swap(pieces[k - low], axis, low * unit))
    return pieces


def tree_sum(parts):
    while len(parts) > 1:
        parts = [parts[i] + parts[i + 1] for i in range(0, len(parts), 2)]
    return parts[0]


def global_rows(index, own, R, C, a, b):
    device, row = index // own, index % own
    return ((((device % R) ^ a) * C) + ((device // R) ^ b)) * own + row


def score_kernel(spans, ti_ref, qi_ref, *refs, n_queries, sizes, first, last, unroll):
    R, C, nt, nq = sizes
    if not first:
        init_ref, *refs = refs
    eig_ref, *refs = refs
    own_ref, other_ref, out_ref, *refs = refs
    if first:
        tiT_ref, *refs = refs
    else:
        tiT_ref = ti_ref
    d_ref, acc_ref = refs
    step = pl.program_id(0)
    a, b = spans[2 * n_queries], spans[2 * n_queries + 1]

    @pl.when(step == 0)
    def _():
        acc_ref[...] = jnp.zeros_like(acc_ref)
        if first:
            tiT_ref[...] = ti_ref[...].T

    d_ref[...] = 1.0 / (eig_ref[...] + damping)
    m = R * (nt + nq)
    tops = [(ref, z * m) for z in range(C // 2) for ref in (own_ref, other_ref)]
    tg = jnp.concatenate([ref[top:top + R * nt, :] for ref, top in tops], axis=0).T.astype(f32)
    qg = jnp.concatenate([ref[top + R * nt:top + m, :] for ref, top in tops], axis=0).T
    pos = global_rows(lax.broadcasted_iota(jnp.int32, (1, R * C * nq), 1), nq, R, C, a, b)

    def one_query(q, carry):
        inside = (pos >= spans[q]) & (pos < spans[n_queries + q])
        mask = jnp.where(inside, 1.0, 0.0).astype(bf16)
        outer = jnp.dot(qg * mask, qi_ref[...], preferred_element_type=f32)
        scaled = (outer * d_ref[...]).astype(bf16)
        paired = jnp.dot(scaled, tiT_ref[...], preferred_element_type=f32)
        v = paired * tg
        acc_ref[q] += v.reshape(v.shape[0] // 8, 8, v.shape[1]).sum(0)
        return carry

    lax.fori_loop(0, n_queries, one_query, 0, unroll=unroll)

    @pl.when(step == pl.num_programs(0) - 1)
    def _():
        total = acc_ref[...].sum(1)
        if not first:
            total = total + init_ref[...]
        if last:
            n = total.shape[1]
            rows = global_rows(lax.broadcasted_iota(jnp.int32, (n, n), 0), nt, R, C, a, b)
            cols = lax.broadcasted_iota(jnp.int32, (n, n), 1)
            onehot = jnp.where(rows == cols, 1.0, 0.0).astype(bf16)
            high = total.astype(bf16)
            rest = total - high.astype(f32)
            middle = rest.astype(bf16)
            low = (rest - middle.astype(f32)).astype(bf16)
            moved = jnp.dot(jnp.concatenate([high, middle, low], axis=0), onehot, preferred_element_type=f32)
            total = moved[:n_queries] + (moved[n_queries:2 * n_queries] + moved[2 * n_queries:])
        out_ref[...] = total


def score(spans, ti, qi, init, eig, own, other, start, n_queries, sizes, last):
    first = init is None
    T, I = ti.shape if first else ti.shape[::-1]
    rows, width = own.shape
    block = math.gcd(256, math.gcd(width, start))
    whole = lambda arr: pl.BlockSpec(arr.shape, lambda i, *_: (0, 0))
    init = [] if first else [init]
    outs = [jax.ShapeDtypeStruct((n_queries, T), f32)]
    if first:
        outs.append(jax.ShapeDtypeStruct((I, T), bf16))
    return pl.pallas_call(
        functools.partial(score_kernel, n_queries=n_queries, sizes=sizes, first=first,
                          last=last, unroll=n_queries),
        out_shape=outs,
        grid_spec=pltpu.PrefetchScalarGridSpec(
            num_scalar_prefetch=1,
            grid=(width // block,),
            in_specs=[
                whole(ti), whole(qi), *map(whole, init),
                pl.BlockSpec((block, I), lambda i, *_: (start // block + i, 0)),
                *[pl.BlockSpec((rows, block), lambda i, *_: (0, i)) for _ in range(2)],
            ],
            out_specs=[whole(o) for o in outs],
            scratch_shapes=[
                pltpu.VMEM((block, I), f32),
                pltpu.VMEM((n_queries, 8, T), f32),
            ],
        ),
        compiler_params=pltpu.CompilerParams(
            dimension_semantics=("arbitrary",), vmem_limit_bytes=56 << 20),
    )(spans, ti, qi, *init, eig, own, other)


def shards(
    train_inputs,
    train_grads,
    query_inputs,
    query_grads,
    input_basis,
    output_basis,
    eigenvalues,
    query_starts,
    query_ends,
):
    R, C = lax.axis_size("row"), lax.axis_size("col")
    Z = C // 2
    a, b = lax.axis_index("row"), lax.axis_index("col")
    nt, nq = train_inputs.shape[0], query_inputs.shape[0]
    n = nt + nq
    K_in, I = input_basis.shape
    K_out, O = output_basis.shape
    n_queries = query_starts.shape[0]

    spans = jnp.concatenate([query_starts, query_ends, jnp.stack([a, b]).astype(jnp.int32)])

    x_in = jnp.concatenate([train_inputs, query_inputs], axis=0)
    in_a = [swap(lax.dynamic_slice_in_dim(x_in, (a ^ k) * K_in, K_in, 1), "row", k) for k in range(R)]
    x_out = jnp.concatenate([train_grads, query_grads], axis=0)
    parts = [lax.dynamic_slice_in_dim(x_out, (b ^ k) * K_out, K_out, 1) for k in range(C)]
    other = swap(jnp.concatenate(parts[1::2], axis=0), "col", 1)
    pairs = [jnp.concatenate([parts[2 * z], other[z * n:(z + 1) * n]], axis=0) for z in range(Z)]
    out_a = [swap(p, "col", 2 * z) for z, p in enumerate(pairs)]

    in_a = jnp.concatenate(in_a, axis=0)
    in_z = gather(in_a, "col", 2)
    in_c = [swap(p, "col", 1) for p in in_z]
    out_a = jnp.concatenate(out_a, axis=0)
    out_r = [swap(out_a, "row", k) for k in range(R)]

    groups = group_ranges(Z)

    def send_inputs(g):
        zs = groups[g]
        pieces = [p for z in zs for p in (in_z[z], in_c[z])]
        rows = jnp.stack([p.reshape(R, n, K_in) for p in pieces], axis=1).reshape(R, 2 * len(zs) * n, K_in)
        parts = []
        for k in range(R):
            parts.append(jnp.dot(rows[k], input_basis, preferred_element_type=f32))
        return [parts[0]] + [swap(parts[k], "row", k) for k in range(1, R)]

    def share_inputs(got):
        total = jnp.concatenate([tree_sum(p).astype(bf16) for p in got], axis=0)
        return [swap(total, "row", k).reshape(-1, n, I) for k in range(R)]

    def grad_rows():
        stacked = jnp.stack(out_r, axis=0).reshape(R, Z, 2, n, K_out)

        def half(rcore):
            h = stacked[:, :, rcore]
            t = h[:, :, :nt].transpose(1, 0, 2, 3).reshape(Z, R * nt, K_out)
            q = h[:, :, nt:].transpose(1, 0, 2, 3).reshape(Z, R * nq, K_out)
            return jnp.concatenate([t, q], axis=1).reshape(Z * R * n, K_out)

        return half(0), half(1)

    starts = [sum(CHUNKS[:c]) * O // sum(CHUNKS) for c in range(len(CHUNKS) + 1)]

    def send_grads(c, mine, other):
        basis = output_basis[:, starts[c]:starts[c + 1]]
        sent = jnp.dot(other, basis, preferred_element_type=f32)
        got = swap(sent, "col", 1)
        kept = jnp.dot(mine, basis, preferred_element_type=f32)
        parts = list((kept + got).reshape(Z, R * n, -1))
        parts = [parts[0]] + [p.astype(bf16) for p in parts[1:]]
        return [swap(p, "col", 2 * z) for z, p in enumerate(parts)]

    def share_grads(got):
        got = [got[0]] + [p.astype(f32) for p in got[1:]]
        own = tree_sum(got).astype(bf16)
        own = jnp.concatenate([swap(own, "col", 2 * z) for z in range(Z)], axis=0)
        return own, swap(own, "col", 1)

    in_got = [send_inputs(g) for g in range(len(GROUPS))]
    mine, other = grad_rows()
    sums = [send_grads(c, mine, other) for c in range(len(CHUNKS))]
    shared = [share_inputs([in_got[g] for g in gs]) for gs in SHARES]
    grad_pieces = [share_grads(got) for got in sums]
    ti = jnp.concatenate([jnp.stack([p[:, :nt] for p in rot], axis=1) for rot in shared], axis=0)
    qi = jnp.concatenate([jnp.stack([p[:, nt:] for p in rot], axis=1) for rot in shared], axis=0)
    ti, qi = ti.reshape(R * C * nt, I), qi.reshape(R * C * nq, I)

    scores = None
    for c in range(len(CHUNKS)):
        scores, *shared = score(spans, ti, qi, scores, eigenvalues, *grad_pieces[c], starts[c], n_queries,
                                (R, C, nt, nq), c == len(CHUNKS) - 1)
        ti = shared[0] if shared else ti

    scores = scores + swap(scores, "col", 1)
    scores = tree_sum([swap(scores, "col", 2 * z) for z in range(Z)])
    scores = tree_sum([swap(scores, "row", k) for k in range(R)])
    return scores * (1.0 / math.sqrt(K_in * R * O * R * QBLOCK))


def group_ranges(Z):
    ends = [sum(GROUPS[:g]) * Z // sum(GROUPS) for g in range(len(GROUPS) + 1)]
    return [range(x, y) for x, y in zip(ends, ends[1:])]


def solution(mesh):
    in_specs = (
        P(("row", "col"), None),
        P(("row", "col"), None),
        P(("row", "col"), None),
        P(("row", "col"), None),
        P("row", "col"),
        P("col", "row"),
        P("row", "col"),
        P(),
        P(),
    )

    return jax.shard_map(shards, mesh=mesh, in_specs=in_specs, out_specs=P(), check_vma=False)
```
